32 devices in a mesh: seq: 8 (over y, x, core), head: 4 (over z).
Axes of the slice: x: 2, y: 2, z: 4, core: 2. Of those that a mesh axis runs over, the one named last changes fastest.
Arguments:
- queries: bfloat16 [2048, 64, 128], P('seq', 'head'), may hold values from -200 to 200
- keys: bfloat16 [2048, 8, 128], P('seq', 'head'), may hold values from -8 to 8
- values: bfloat16 [2048, 8, 128], P('seq', 'head'), may hold values from -6 to 6
- query_map: bfloat16 [64, 128, 64], P('head'), may hold values from -40 to 40
- key_map: bfloat16 [8, 128, 64], P('head'), may hold values from -40 to 40
Outputs:
- teacher_attn: bfloat16 [2048, 64, 128], P('seq', 'head')
- student_attn: bfloat16 [2048, 64, 128], P('seq', 'head')
- loss: float32 [], replicated
The draws below stay inside these ranges and needn't reach their ends.
All inputs are finite; a program needn't handle non-finite values.
Results may differ from the reference program's by a relative error of at most 0.01.
Values may be sent and summed in bfloat16 or wider, within the bound.
A program may use at most 320 MiB of HBM per device.

```python
import jax
import jax.numpy as jnp
from jax import lax

H = 64
KV = 8
HD = 128
FH = 64
TOK_DEV = 256
FEAT = 128
SEQ_LEN = 2048


def query_key_pair(key):
    split_keys = jax.random.split(jax.random.fold_in(key, 7), 2)
    keys = jax.random.normal(split_keys[1], (SEQ_LEN, KV, HD), jnp.float32)
    queries = jax.random.normal(split_keys[0], (SEQ_LEN, H, HD), jnp.float32)
    return (queries, keys)


def feature_map(key, heads):
    split_keys = jax.random.split(key, 1)
    weights = jax.random.normal(split_keys[0], (heads, HD, FH), jnp.float32) / HD ** 0.5
    return weights


def draw_queries(key, part):
    return query_key_pair(key)[0].astype(jnp.bfloat16)


def draw_keys(key, part):
    return query_key_pair(key)[1].astype(jnp.bfloat16)


def draw_query_map(key, part):
    return feature_map(jax.random.fold_in(key, 11), H).astype(jnp.bfloat16)


def draw_key_map(key, part):
    return feature_map(jax.random.fold_in(key, 13), KV).astype(jnp.bfloat16)


def steps_of(own_key, shape, cuts, low, high):
    def one(dim, shards_of):
        heights = jax.random.uniform(jax.random.fold_in(jax.random.fold_in(own_key, 6), dim), (shards_of,), jnp.float32, low / len(cuts), high / len(cuts))
        return jnp.repeat(jnp.exp(heights), shape[dim] // shards_of).reshape((-1,) + (1,) * (len(shape) - dim - 1))

    level = one(*cuts[0])
    for cut in cuts[1:]:
        level = level * one(*cut)
    return level


def centred(key, shape, scale, reach, cuts=(), held_as=jnp.bfloat16):
    array = jax.random.normal(key, shape, jnp.float32) * scale
    if len(cuts) > 0:
        array = steps_of(key, shape, cuts, -0.22, 0.18) * array
    return jnp.clip(array, min=-reach, max=reach).astype(held_as)


def setup_inputs(seed: int = 0) -> dict:
    seeds = jax.random.split(jax.random.key(seed), 6)
    queries = draw_queries(jax.random.fold_in(seeds[5], 71), 0)
    keys = draw_keys(jax.random.fold_in(seeds[5], 71), 0)
    values = centred(seeds[2], (SEQ_LEN, KV, HD), 1.0, 6.0, ((0, 8), (1, 4)))
    query_map = draw_query_map(jax.random.fold_in(seeds[5], 71), 0)
    key_map = draw_key_map(jax.random.fold_in(seeds[5], 71), 0)
    return dict(queries=queries, keys=keys, values=values, query_map=query_map, key_map=key_map)


def features(rows, projection):
    mapped = jnp.einsum('thd,hdf->thf', rows.astype(jnp.float32), projection.astype(jnp.float32))
    both = jnp.concatenate([jax.nn.softmax(mapped, axis=-1), jax.nn.softmax(-mapped, axis=-1)], axis=-1)
    return both.astype(jnp.bfloat16)


def teacher(queries, keys, values):
    group = H // KV
    block = min(512, SEQ_LEN)
    count = SEQ_LEN // block
    scale = 1.0 / (HD ** 0.5)
    grouped = queries.reshape(SEQ_LEN, KV, group, HD).transpose(1, 0, 2, 3).astype(jnp.float32)
    key_rows = keys.transpose(1, 0, 2).astype(jnp.float32)
    value_rows = values.transpose(1, 0, 2).astype(jnp.float32)
    key_pos = jnp.arange(SEQ_LEN, dtype=jnp.int32)

    def single(index):
        head_group = index // count
        first = (index % count) * block
        query_block = lax.dynamic_slice_in_dim(grouped[head_group], first, block, 0)
        scores = jnp.einsum('qsd,kd->sqk', query_block, key_rows[head_group]) * scale
        query_pos = first + jnp.arange(block, dtype=jnp.int32)
        allowed = query_pos[:, None] >= key_pos[None, :]
        scores = jnp.where(allowed[None], scores, -1e30)
        top = jnp.max(scores, axis=-1, keepdims=True)
        weight = jnp.where(allowed[None], jnp.exp(scores - top), 0.0)
        total = jnp.sum(weight, axis=-1)
        mixed = jnp.einsum('sqk,kd->qsd', weight.astype(jnp.bfloat16).astype(jnp.float32), value_rows[head_group])
        return mixed / total.T[:, :, None]

    pieces = lax.map(single, jnp.arange(KV * count, dtype=jnp.int32))
    pieces = pieces.reshape(KV, count, block, group, HD).transpose(1, 2, 0, 3, 4)
    return pieces.reshape(SEQ_LEN, H, HD).astype(jnp.bfloat16)


def student(queries, keys, values, query_map, key_map):
    group = H // KV
    blocks = SEQ_LEN // TOK_DEV
    phi_q = features(queries, query_map).reshape(blocks, TOK_DEV, KV, group, FEAT)
    phi_k = features(keys, key_map).reshape(blocks, TOK_DEV, KV, FEAT)
    value_blocks = values.reshape(blocks, TOK_DEV, KV, HD)
    lower = jnp.tril(jnp.ones((TOK_DEV, TOK_DEV), dtype=bool))

    def advance(carry, inputs):
        state, norm = carry
        pq, pk, vb = inputs
        pqf = pq.astype(jnp.float32)
        pkf = pk.astype(jnp.float32)
        vbf = vb.astype(jnp.float32)
        inner = jnp.einsum('cgsf,egf->gsce', pqf, pkf)
        inner = jnp.where(lower[None, None], inner, 0.0)
        den_local = jnp.sum(inner, axis=-1)
        num_local = jnp.einsum('gsce,egd->cgsd', inner.astype(jnp.bfloat16).astype(jnp.float32), vbf)
        state_round = lax.optimization_barrier(state.astype(jnp.bfloat16)).astype(jnp.float32)
        num_prev = jnp.einsum('cgsf,gfd->cgsd', pqf, state_round)
        den_prev = jnp.einsum('cgsf,gf->gsc', pqf, norm, precision=lax.Precision.HIGHEST)
        denom = (den_local + den_prev).transpose(2, 0, 1)[..., None]
        result = ((num_local + num_prev) / denom).astype(jnp.bfloat16)
        state = state + jnp.einsum('cgf,cgd->gfd', pkf, vbf)
        norm = norm + jnp.sum(pkf, axis=0)
        return (state, norm), result

    start = (jnp.zeros((KV, FEAT, HD), jnp.float32), jnp.zeros((KV, FEAT), jnp.float32))
    _, outputs = lax.scan(advance, start, (phi_q, phi_k, value_blocks))
    return outputs.reshape(SEQ_LEN, H, HD)


def reference(queries, keys, values, query_map, key_map):
    teacher_attn = teacher(queries, keys, values)
    student_attn = student(queries, keys, values, query_map, key_map)
    diff = teacher_attn.astype(jnp.float32) - student_attn.astype(jnp.float32)
    loss = jnp.sum(diff * diff) / (SEQ_LEN * H * HD)
    return teacher_attn, student_attn, loss
```

```python
import functools
import math

import jax
import jax.numpy as jnp
from jax import lax
from jax.experimental import pallas as pl
from jax.experimental.pallas import tpu as pltpu
from jax.sharding import PartitionSpec as P

MESH = pl.DeviceIdType.MESH
NT = (((1,), (1,)), ((), ()))
NN = (((1,), (0,)), ((), ()))
LOW = -1e30


def mm(a, b, dims=NN):
    return lax.dot_general(a, b, dims, preferred_element_type=jnp.float32)


def kernel(
    n,
    m,
    count,
    q_ref,
    kv_ref,
    qm_ref,
    km_ref,
    t_ref,
    s_ref,
    loss_ref,
    kvbuf,
    wide,
    qh,
    phiq,
    top,
    acc,
    sacc,
    state,
    kmt,
    slots1,
    slots2,
    send_sem,
    fwd_sem,
    recv_sem,
    l1_send,
    l1_recv,
    l2_send,
    l2_recv,
):
    rows, heads, d = q_ref.shape
    kvh = kv_ref.shape[0] // 2
    group = heads // kvh
    f = qm_ref.shape[2]
    c2 = math.log2(math.e) / math.sqrt(d)
    p = lax.axis_index("seq")
    hid = lax.axis_index("head")
    chip = p // 2
    core = p % 2
    partner = p + 1 - 2 * core
    chips = n // 2

    barrier = pltpu.get_barrier_semaphore()
    for off in range(1, n):
        pl.semaphore_signal(
            barrier, inc=1, device_id={"seq": lax.rem(p + off, n)}, device_id_type=MESH
        )
    for off in range(1, m):
        pl.semaphore_signal(
            barrier, inc=1, device_id={"head": lax.rem(hid + off, m)}, device_id_type=MESH
        )

    wide[...] = q_ref[...].astype(jnp.float32).reshape(rows * heads, d)
    for h in range(heads):
        qh[h] = wide[pl.ds(h, rows, stride=heads), :].astype(jnp.bfloat16)
    for g in range(kvh):
        km = km_ref[g].astype(jnp.float32)
        kmt[g] = jnp.concatenate([km, -km], axis=1).T.astype(jnp.bfloat16)

    pl.semaphore_wait(barrier, n - 1 + m - 1)

    def direct(to_chip):
        return pltpu.make_async_remote_copy(
            src_ref=kv_ref,
            dst_ref=kvbuf.at[p],
            send_sem=send_sem.at[to_chip],
            recv_sem=recv_sem.at[p],
            device_id={"seq": to_chip * 2 + core},
            device_id_type=MESH,
        )

    def to_partner():
        return pltpu.make_async_remote_copy(
            src_ref=kv_ref,
            dst_ref=kvbuf.at[p],
            send_sem=send_sem.at[chip],
            recv_sem=recv_sem.at[p],
            device_id={"seq": partner},
            device_id_type=MESH,
        )

    def forward(from_chip):
        block = from_chip * 2 + core
        return pltpu.make_async_remote_copy(
            src_ref=kvbuf.at[block],
            dst_ref=kvbuf.at[block],
            send_sem=fwd_sem.at[from_chip],
            recv_sem=recv_sem.at[block],
            device_id={"seq": partner},
            device_id_type=MESH,
        )

    def arrived(block):
        pltpu.make_async_remote_copy(
            src_ref=kvbuf.at[block],
            dst_ref=kvbuf.at[block],
            send_sem=fwd_sem.at[0],
            recv_sem=recv_sem.at[block],
            device_id={"seq": partner},
            device_id_type=MESH,
        ).wait_recv()

    def each_later(act):
        def body(i, carry):
            act(direct(i))
            return carry

        lax.fori_loop(chip + 1, chips, body, 0)

    each_later(lambda copy: copy.start())

    @pl.when(core == 0)
    def _():
        to_partner().start()

    ones = jnp.ones((rows, d), jnp.bfloat16)

    def key_features(k, g):
        u = mm(kmt[g], k, NT)
        parts = []
        for half in (u[:f], u[f:]):
            e = jnp.exp(half - jnp.max(half, axis=0, keepdims=True))
            parts.append(e / jnp.sum(e, axis=0, keepdims=True))
        return jnp.concatenate(parts, axis=0).astype(jnp.bfloat16)

    lower = lax.broadcasted_iota(jnp.int32, (rows, rows), 0) >= lax.broadcasted_iota(
        jnp.int32, (rows, rows), 1
    )
    left = lax.broadcasted_iota(jnp.int32, (rows, 2 * f), 1) < f
    for g in range(kvh):
        k = kv_ref[g]
        v1 = jnp.concatenate([kv_ref[kvh + g], ones], axis=1)
        phik = key_features(k, g)
        state[g] = jnp.zeros_like(state[g])
        for h in range(g * group, (g + 1) * group):
            q = qh[h]
            s = jnp.where(lower, mm(q, k, NT), LOW)
            high = jnp.max(s, axis=1, keepdims=True)
            w = jnp.exp2((s - high) * c2).astype(jnp.bfloat16)
            top[h] = jnp.broadcast_to(high, (rows, d))
            acc[h] = mm(w, v1)
            qm = qm_ref[h]
            u = mm(q, jnp.concatenate([qm, -qm], axis=1))
            m1 = jnp.max(jnp.where(left, u, -jnp.inf), axis=1, keepdims=True)
            m2 = jnp.max(jnp.where(left, -jnp.inf, u), axis=1, keepdims=True)
            e = jnp.exp(u - jnp.where(left, m1, m2))
            z1 = jnp.sum(jnp.where(left, e, 0.0), axis=1, keepdims=True)
            z2 = jnp.sum(jnp.where(left, 0.0, e), axis=1, keepdims=True)
            phi = (e / jnp.where(left, z1, z2)).astype(jnp.bfloat16)
            phiq[h] = phi
            a = jnp.where(lower, mm(phi, phik), 0.0).astype(jnp.bfloat16)
            sacc[h] = mm(a, v1)

    def step(blocks):
        for g in range(kvh):
            k = jnp.concatenate([kvbuf[b, g] for b in blocks], axis=0)
            v = jnp.concatenate([kvbuf[b, kvh + g] for b in blocks], axis=0)
            v1 = jnp.concatenate([v, jnp.ones_like(v)], axis=1)
            state[g] += mm(key_features(k, g), v1)
            for h in range(g * group, (g + 1) * group):
                s = mm(qh[h], k, NT)
                before = top[h]
                high = jnp.maximum(before, jnp.max(s, axis=1, keepdims=True))
                top[h] = high
                w = jnp.exp2((s - jnp.concatenate([high] * (s.shape[1] // d), axis=1)) * c2)
                fade = jnp.exp2((before - high) * c2)
                acc[h] = acc[h] * jnp.concatenate([fade, fade], axis=1) + mm(
                    w.astype(jnp.bfloat16), v1
                )

    @pl.when(core == 1)
    def _():
        arrived(p - 1)
        step([p - 1])

    def chip_step(i, carry):
        other = chip - 1 - i
        arrived(other * 2 + core)
        forward(other).start()
        arrived(other * 2 + 1 - core)
        step([other * 2, other * 2 + 1])
        return carry

    lax.fori_loop(0, chip, chip_step, 0)

    part = jnp.zeros((8, d), jnp.float32)
    for h in range(heads):
        a = acc[h]
        wide[pl.ds(h, rows, stride=heads), :] = a[:, :d] / a[:, d:]
    teacher = wide[...].astype(jnp.bfloat16)
    t_ref[...] = teacher.reshape(rows, heads, d)
    for h in range(heads):
        st = state[h // group].astype(jnp.bfloat16)
        a = sacc[h] + mm(phiq[h], st)
        wide[pl.ds(h, rows, stride=heads), :] = a[:, :d] / a[:, d:]
    student = wide[...].astype(jnp.bfloat16)
    s_ref[...] = student.reshape(rows, heads, d)
    diff = t_ref[...].astype(jnp.float32) - s_ref[...].astype(jnp.float32)
    part = jnp.sum((diff * diff).reshape(rows * heads // 8, 8, d), axis=0)

    def exchange(slots, me, size, axis, send, recv, value):
        slots[me] = value

        def copy(off):
            return pltpu.make_async_remote_copy(
                src_ref=slots.at[me],
                dst_ref=slots.at[me],
                send_sem=send.at[off],
                recv_sem=recv.at[off],
                device_id={axis: lax.rem(me + off, size)},
                device_id_type=MESH,
            )

        def landed(off):
            src = lax.rem(me + size - off, size)
            pltpu.make_async_remote_copy(
                src_ref=slots.at[src],
                dst_ref=slots.at[src],
                send_sem=send.at[off],
                recv_sem=recv.at[off],
                device_id={axis: lax.rem(me + off, size)},
                device_id_type=MESH,
            ).wait_recv()

        for off in range(1, size):
            copy(off).start()
        for off in range(1, size):
            landed(off)
        total = slots[0]
        for j in range(1, size):
            total = total + slots[j]
        return total, lambda: [copy(off).wait_send() for off in range(1, size)]

    total, end1 = exchange(slots1, p, n, "seq", l1_send, l1_recv, part)
    total, end2 = exchange(slots2, hid, m, "head", l2_send, l2_recv, total)
    loss_ref[0, 0] = jnp.sum(total) * (1.0 / count)

    end1()
    end2()
    each_later(lambda copy: copy.wait_send())

    @pl.when(core == 0)
    def _():
        to_partner().wait_send()

    def sent(i, carry):
        forward(chip - 1 - i).wait_send()
        return carry

    lax.fori_loop(0, chip, sent, 0)


def local(queries, keys, values, query_map, key_map):
    rows, heads, d = queries.shape
    kvh = keys.shape[1]
    n, m = lax.axis_size("seq"), lax.axis_size("head")
    f = query_map.shape[2]
    count = rows * n * heads * m * d
    kv = jnp.concatenate([keys.transpose(1, 0, 2), values.transpose(1, 0, 2)], axis=0)
    vmem = pl.BlockSpec(memory_space=pltpu.VMEM)
    dma = pltpu.SemaphoreType.DMA
    t, s, loss = pl.pallas_call(
        functools.partial(kernel, n, m, count),
        out_shape=(
            jax.ShapeDtypeStruct(queries.shape, jnp.bfloat16),
            jax.ShapeDtypeStruct(queries.shape, jnp.bfloat16),
            jax.ShapeDtypeStruct((1, 1), jnp.float32),
        ),
        in_specs=[vmem] * 4,
        out_specs=(vmem, vmem, pl.BlockSpec(memory_space=pltpu.SMEM)),
        scratch_shapes=[
            pltpu.VMEM((n, 2 * kvh, rows, d), jnp.bfloat16),
            pltpu.VMEM((rows * heads, d), jnp.float32),
            pltpu.VMEM((heads, rows, d), jnp.bfloat16),
            pltpu.VMEM((heads, rows, 2 * f), jnp.bfloat16),
            pltpu.VMEM((heads, rows, d), jnp.float32),
            pltpu.VMEM((heads, rows, 2 * d), jnp.float32),
            pltpu.VMEM((heads, rows, 2 * d), jnp.float32),
            pltpu.VMEM((kvh, 2 * f, 2 * d), jnp.float32),
            pltpu.VMEM((kvh, 2 * f, d), jnp.bfloat16),
            pltpu.VMEM((n, 8, d), jnp.float32),
            pltpu.VMEM((m, 8, d), jnp.float32),
            dma((n // 2,)),
            dma((n // 2,)),
            dma((n,)),
            dma((n,)),
            dma((n,)),
            dma((m,)),
            dma((m,)),
        ],
        compiler_params=pltpu.CompilerParams(
            collective_id=0, has_side_effects=True, vmem_limit_bytes=60 * 2**20
        ),
    )(queries, kv, query_map, key_map)
    return t, s, loss.reshape(())


def solution(mesh):
    placed = (
        P("seq", "head", None),
        P("seq", "head", None),
        P("seq", "head", None),
        P("head", None, None),
        P("head", None, None),
    )
    return jax.shard_map(
        local,
        mesh=mesh,
        in_specs=placed,
        out_specs=(P("seq", "head", None), P("seq", "head", None), P()),
        check_vma=False,
    )
```

```python
import functools
import math

import jax
import jax.numpy as jnp
from jax import lax
from jax.experimental import pallas as pl
from jax.experimental.pallas import tpu as pltpu
from jax.sharding import PartitionSpec as P

MESH = pl.DeviceIdType.MESH
NT = (((1,), (1,)), ((), ()))
NN = (((1,), (0,)), ((), ()))
LOW = -1e30


def mm(a, b, dims=NN):
    return lax.dot_general(a, b, dims, preferred_element_type=jnp.float32)


def kernel(
    n,
    m,
    count,
    q_ref,
    k_ref,
    v_ref,
    qm_ref,
    km_ref,
    t_ref,
    s_ref,
    loss_ref,
    kvbuf,
    wide,
    qh,
    phiq,
    top,
    acc,
    sacc,
    state,
    slots1,
    slots2,
    send_sem,
    fwd_sem,
    recv_sem,
    l1_send,
    l1_recv,
    l2_send,
    l2_recv,
):
    rows, heads, d = q_ref.shape
    kvh = k_ref.shape[0]
    group = heads // kvh
    f = qm_ref.shape[1]
    c2 = math.log2(math.e) / math.sqrt(d)
    p = lax.axis_index("seq")
    hid = lax.axis_index("head")
    chip = p // 2
    core = p % 2
    partner = p + 1 - 2 * core
    chips = n // 2

    barrier = pltpu.get_barrier_semaphore()
    for off in range(1, n):
        pl.semaphore_signal(
            barrier, inc=1, device_id={"seq": lax.rem(p + off, n)}, device_id_type=MESH
        )
    for off in range(1, m):
        pl.semaphore_signal(
            barrier, inc=1, device_id={"head": lax.rem(hid + off, m)}, device_id_type=MESH
        )

    wide[...] = q_ref[...].astype(jnp.float32).reshape(rows * heads, d)
    for h in range(heads):
        qh[h] = wide[pl.ds(h, rows, stride=heads), :].astype(jnp.bfloat16)

    pl.semaphore_wait(barrier, n - 1 + m - 1)

    def own(part, device, sem):
        return pltpu.make_async_remote_copy(
            src_ref=(k_ref, v_ref)[part],
            dst_ref=kvbuf.at[p, part],
            send_sem=send_sem.at[part, sem],
            recv_sem=recv_sem.at[part, p],
            device_id={"seq": device},
            device_id_type=MESH,
        )

    def forward(part, from_chip):
        block = from_chip * 2 + core
        return pltpu.make_async_remote_copy(
            src_ref=kvbuf.at[block, part],
            dst_ref=kvbuf.at[block, part],
            send_sem=fwd_sem.at[part, from_chip],
            recv_sem=recv_sem.at[part, block],
            device_id={"seq": partner},
            device_id_type=MESH,
        )

    def arrived(part, block):
        pltpu.make_async_remote_copy(
            src_ref=kvbuf.at[block, part],
            dst_ref=kvbuf.at[block, part],
            send_sem=fwd_sem.at[part, 0],
            recv_sem=recv_sem.at[part, block],
            device_id={"seq": partner},
            device_id_type=MESH,
        ).wait_recv()

    def each_own(act):
        @pl.when(core == 0)
        def _():
            act(own(0, partner, chip))
            act(own(1, partner, chip))

        def body(i, carry):
            act(own(0, i * 2 + core, i))
            act(own(1, i * 2 + core, i))
            return carry

        lax.fori_loop(chip + 1, chips, body, 0)

    each_own(lambda copy: copy.start())

    ones = jnp.ones((rows, d), jnp.bfloat16)

    def features(x, half_map):
        u = mm(jnp.concatenate([half_map, -half_map], axis=0), x, NT)
        parts = []
        for half in (u[:f], u[f:]):
            e = jnp.exp(half - jnp.max(half, axis=0, keepdims=True))
            parts.append(e * (1.0 / jnp.sum(e, axis=0, keepdims=True)))
        return jnp.concatenate(parts, axis=0)

    def key_features(k, g):
        return features(k, km_ref[g]).astype(jnp.bfloat16)

    lower = lax.broadcasted_iota(jnp.int32, (rows, rows), 0) >= lax.broadcasted_iota(
        jnp.int32, (rows, rows), 1
    )
    for g in range(kvh):
        k = k_ref[g]
        v1 = jnp.concatenate([v_ref[g], ones], axis=1)
        phik = key_features(k, g)
        state[g] = jnp.zeros_like(state[g])
        for h in range(g * group, (g + 1) * group):
            q = qh[h]
            s = jnp.where(lower, mm(q, k, NT), LOW)
            high = jnp.max(s, axis=1, keepdims=True)
            w = jnp.exp2((s - high) * c2).astype(jnp.bfloat16)
            top[h] = jnp.broadcast_to(high, (rows, d))
            acc[h] = mm(w, v1)
            phi = features(q, qm_ref[h]).T.astype(jnp.bfloat16)
            phiq[h] = phi
            a = jnp.where(lower, mm(phi, phik), 0.0).astype(jnp.bfloat16)
            sacc[h] = mm(a, v1)

    def step(blocks):
        for g in range(kvh):
            k = jnp.concatenate([kvbuf[b, 0, g] for b in blocks], axis=0)
            v = jnp.concatenate([kvbuf[b, 1, g] for b in blocks], axis=0)
            v1 = jnp.concatenate([v, jnp.ones_like(v)], axis=1)
            state[g] += mm(key_features(k, g), v1)
            for h in range(g * group, (g + 1) * group):
                s = mm(qh[h], k, NT)
                before = top[h]
                high = jnp.maximum(before, jnp.max(s, axis=1, keepdims=True))
                top[h] = high
                w = jnp.exp2((s - jnp.concatenate([high] * (s.shape[1] // d), axis=1)) * c2)
                fade = jnp.exp2((before - high) * c2)
                acc[h] = acc[h] * jnp.concatenate([fade, fade], axis=1) + mm(
                    w.astype(jnp.bfloat16), v1
                )

    @pl.when(core == 1)
    def _():
        for part in range(2):
            arrived(part, p - 1)
        step([p - 1])

    def chip_step(i, carry):
        other = chip - 1 - i
        for part in range(2):
            arrived(part, other * 2 + core)
            forward(part, other).start()
        for part in range(2):
            arrived(part, other * 2 + 1 - core)
        step([other * 2, other * 2 + 1])
        return carry

    lax.fori_loop(0, chip, chip_step, 0)

    part = jnp.zeros((8, d), jnp.float32)
    for h in range(heads):
        a = acc[h]
        t = (a[:, :d] / a[:, d:]).astype(jnp.bfloat16)
        t_ref[h] = t
        b = sacc[h] + mm(phiq[h], state[h // group].astype(jnp.bfloat16))
        o = (b[:, :d] / b[:, d:]).astype(jnp.bfloat16)
        s_ref[h] = o
        diff = t.astype(jnp.float32) - o.astype(jnp.float32)
        part += jnp.sum((diff * diff).reshape(rows // 8, 8, d), axis=0)

    def exchange(slots, me, size, axis, send, recv, value):
        slots[me] = value

        def copy(off):
            return pltpu.make_async_remote_copy(
                src_ref=slots.at[me],
                dst_ref=slots.at[me],
                send_sem=send.at[off],
                recv_sem=recv.at[off],
                device_id={axis: lax.rem(me + off, size)},
                device_id_type=MESH,
            )

        def landed(off):
            src = lax.rem(me + size - off, size)
            pltpu.make_async_remote_copy(
                src_ref=slots.at[src],
                dst_ref=slots.at[src],
                send_sem=send.at[off],
                recv_sem=recv.at[off],
                device_id={axis: lax.rem(me + off, size)},
                device_id_type=MESH,
            ).wait_recv()

        for off in range(1, size):
            copy(off).start()
        for off in range(1, size):
            landed(off)
        total = slots[0]
        for j in range(1, size):
            total = total + slots[j]
        return total, lambda: [copy(off).wait_send() for off in range(1, size)]

    total, end1 = exchange(slots1, p, n, "seq", l1_send, l1_recv, part)
    total, end2 = exchange(slots2, hid, m, "head", l2_send, l2_recv, total)
    loss_ref[0, 0] = jnp.sum(total) * (1.0 / count)

    end1()
    end2()
    each_own(lambda copy: copy.wait_send())

    def sent(i, carry):
        for part in range(2):
            forward(part, chip - 1 - i).wait_send()
        return carry

    lax.fori_loop(0, chip, sent, 0)


def local(queries, keys, values, query_map, key_map):
    rows, heads, d = queries.shape
    kvh = keys.shape[1]
    n, m = lax.axis_size("seq"), lax.axis_size("head")
    f = query_map.shape[2]
    count = rows * n * heads * m * d
    vmem = pl.BlockSpec(memory_space=pltpu.VMEM)
    dma = pltpu.SemaphoreType.DMA
    t, s, loss = pl.pallas_call(
        functools.partial(kernel, n, m, count),
        out_shape=(
            jax.ShapeDtypeStruct((heads, rows, d), jnp.bfloat16),
            jax.ShapeDtypeStruct((heads, rows, d), jnp.bfloat16),
            jax.ShapeDtypeStruct((1, 1), jnp.float32),
        ),
        in_specs=[vmem] * 5,
        out_specs=(vmem, vmem, pl.BlockSpec(memory_space=pltpu.SMEM)),
        scratch_shapes=[
            pltpu.VMEM((n, 2, kvh, rows, d), jnp.bfloat16),
            pltpu.VMEM((rows * heads, d), jnp.float32),
            pltpu.VMEM((heads, rows, d), jnp.bfloat16),
            pltpu.VMEM((heads, rows, 2 * f), jnp.bfloat16),
            pltpu.VMEM((heads, rows, d), jnp.float32),
            pltpu.VMEM((heads, rows, 2 * d), jnp.float32),
            pltpu.VMEM((heads, rows, 2 * d), jnp.float32),
            pltpu.VMEM((kvh, 2 * f, 2 * d), jnp.float32),
            pltpu.VMEM((n, 8, d), jnp.float32),
            pltpu.VMEM((m, 8, d), jnp.float32),
            dma((2, n // 2)),
            dma((2, n // 2)),
            dma((2, n)),
            dma((n,)),
            dma((n,)),
            dma((m,)),
            dma((m,)),
        ],
        compiler_params=pltpu.CompilerParams(
            collective_id=0, has_side_effects=True, vmem_limit_bytes=60 * 2**20
        ),
    )(
        queries,
        keys.transpose(1, 0, 2),
        values.transpose(1, 0, 2),
        query_map.transpose(0, 2, 1),
        key_map.transpose(0, 2, 1),
    )
    return t.transpose(1, 0, 2), s.transpose(1, 0, 2), loss.reshape(())


def solution(mesh):
    placed = (
        P("seq", "head", None),
        P("seq", "head", None),
        P("seq", "head", None),
        P("head", None, None),
        P("head", None, None),
    )
    return jax.shard_map(
        local,
        mesh=mesh,
        in_specs=placed,
        out_specs=(P("seq", "head", None), P("seq", "head", None), P()),
        check_vma=False,
    )
```

```python
import functools
import math

import jax
import jax.numpy as jnp
from jax import lax
from jax.experimental import pallas as pl
from jax.experimental.pallas import tpu as pltpu
from jax.sharding import PartitionSpec as P

MESH = pl.DeviceIdType.MESH
NT = (((1,), (1,)), ((), ()))
NN = (((1,), (0,)), ((), ()))
LOW = -1e30


def mm(a, b, dims=NN):
    return lax.dot_general(a, b, dims, preferred_element_type=jnp.float32)


def kernel(
    n,
    m,
    count,
    q_hbm,
    k_ref,
    v_ref,
    qm_ref,
    km_ref,
    t_ref,
    s_ref,
    loss_ref,
    q_ref,
    kvbuf,
    wide,
    qh,
    phiq,
    top,
    acc,
    sacc,
    state,
    slots1,
    slots2,
    send_sem,
    fwd_sem,
    relay_sem,
    local_sem,
    recv_sem,
    l1_send,
    l1_recv,
    l2_send,
    l2_recv,
):
    rows, heads, d = q_ref.shape
    load_q = pltpu.make_async_copy(q_hbm, q_ref, local_sem.at[0])
    load_q.start()
    kvh = k_ref.shape[0]
    group = heads // kvh
    f = qm_ref.shape[1]
    c2 = math.log2(math.e) / math.sqrt(d)
    p = lax.axis_index("seq")
    hid = lax.axis_index("head")
    chip = p // 2
    core = p % 2
    partner = p + 1 - 2 * core
    chips = n // 2
    square = chips == 4

    barrier = pltpu.get_barrier_semaphore()
    for off in range(1, n):
        pl.semaphore_signal(
            barrier, inc=1, device_id={"seq": lax.rem(p + off, n)}, device_id_type=MESH
        )
    for off in range(1, m):
        pl.semaphore_signal(
            barrier, inc=1, device_id={"head": lax.rem(hid + off, m)}, device_id_type=MESH
        )

    def features(x, half_map):
        u = mm(jnp.concatenate([half_map, -half_map], axis=0), x, NT)
        parts = []
        for half in (u[:f], u[f:]):
            e = jnp.exp(half - jnp.max(half, axis=0, keepdims=True))
            parts.append(e * (1.0 / jnp.sum(e, axis=0, keepdims=True)))
        return jnp.concatenate(parts, axis=0)

    load_q.wait()
    wide[...] = q_ref[...].astype(jnp.float32).reshape(rows * heads, d)
    for h in range(heads):
        qh[h] = wide[pl.ds(h, rows, stride=heads), :].astype(jnp.bfloat16)
    for h in range(heads):
        phiq[h] = features(qh[h], qm_ref[h]).T.astype(jnp.bfloat16)

    pl.semaphore_wait(barrier, n - 1 + m - 1)

    def own(part, device, sem):
        return pltpu.make_async_remote_copy(
            src_ref=(k_ref, v_ref)[part],
            dst_ref=kvbuf.at[p, part],
            send_sem=send_sem.at[part, sem],
            recv_sem=recv_sem.at[part, p],
            device_id={"seq": device},
            device_id_type=MESH,
        )

    def forward(part, from_chip):
        block = from_chip * 2 + core
        return pltpu.make_async_remote_copy(
            src_ref=kvbuf.at[block, part],
            dst_ref=kvbuf.at[block, part],
            send_sem=fwd_sem.at[part, from_chip],
            recv_sem=recv_sem.at[part, block],
            device_id={"seq": partner},
            device_id_type=MESH,
        )

    def arrived(part, block):
        pltpu.make_async_remote_copy(
            src_ref=kvbuf.at[block, part],
            dst_ref=kvbuf.at[block, part],
            send_sem=fwd_sem.at[part, 0],
            recv_sem=recv_sem.at[part, block],
            device_id={"seq": partner},
            device_id_type=MESH,
        ).wait_recv()

    def near(to):
        if to == 0:
            return (chip == 1) & (core == 0)
        if to == 3:
            return (chip == 1) | (chip == 2)
        return chip == 0

    def relay(part, block, to_chip):
        return pltpu.make_async_remote_copy(
            src_ref=kvbuf.at[block, part],
            dst_ref=kvbuf.at[block, part],
            send_sem=relay_sem.at[part],
            recv_sem=recv_sem.at[part, block],
            device_id={"seq": to_chip * 2 + core},
            device_id_type=MESH,
        )

    relays = ((0, 0, 1, 2), (1, 0, 0, 3), (2, 1, 0, 3), (3, 1, 1, 2))

    def each_own(act):
        @pl.when(core == 0)
        def _():
            act(own(0, partner, chip))
            act(own(1, partner, chip))

        if square:
            for to in range(4):

                @pl.when(near(to))
                def _():
                    act(own(0, to * 2 + core, to))
                    act(own(1, to * 2 + core, to))

            return

        def body(i, carry):
            act(own(0, i * 2 + core, i))
            act(own(1, i * 2 + core, i))
            return carry

        lax.fori_loop(chip + 1, chips, body, 0)

    each_own(lambda copy: copy.start())

    ones = jnp.ones((rows, d), jnp.bfloat16)

    def key_features(k, g):
        return features(k, km_ref[g]).astype(jnp.bfloat16)

    lower = lax.broadcasted_iota(jnp.int32, (rows, rows), 0) >= lax.broadcasted_iota(
        jnp.int32, (rows, rows), 1
    )
    for g in range(kvh):
        k = k_ref[g]
        v1 = jnp.concatenate([v_ref[g], ones], axis=1)
        phik = key_features(k, g)
        state[g] = jnp.zeros_like(state[g])
        for h in range(g * group, (g + 1) * group):
            q = qh[h]
            s = jnp.where(lower, mm(q, k, NT), LOW)
            high = jnp.max(s, axis=1, keepdims=True)
            w = jnp.exp2((s - high) * c2).astype(jnp.bfloat16)
            top[h] = jnp.broadcast_to(high, (rows, d))
            acc[h] = mm(w, v1)
            a = jnp.where(lower, mm(phiq[h], phik), 0.0).astype(jnp.bfloat16)
            sacc[h] = mm(a, v1)

    def step(blocks):
        for g in range(kvh):
            k = jnp.concatenate([kvbuf[b, 0, g] for b in blocks], axis=0)
            v = jnp.concatenate([kvbuf[b, 1, g] for b in blocks], axis=0)
            v1 = jnp.concatenate([v, jnp.ones_like(v)], axis=1)
            state[g] += mm(key_features(k, g), v1)
            for h in range(g * group, (g + 1) * group):
                s = mm(qh[h], k, NT)
                before = top[h]
                high = jnp.maximum(before, jnp.max(s, axis=1, keepdims=True))
                top[h] = high
                w = jnp.exp2((s - jnp.concatenate([high] * (s.shape[1] // d), axis=1)) * c2)
                fade = jnp.exp2((before - high) * c2)
                acc[h] = acc[h] * jnp.concatenate([fade, fade], axis=1) + mm(
                    w.astype(jnp.bfloat16), v1
                )

    @pl.when(core == 1)
    def _():
        for part in range(2):
            arrived(part, p - 1)
        step([p - 1])

    def each_relay(origin, part, act):
        for who, lane, source, to in relays:

            @pl.when((chip == who) & (core == lane) & (origin == source))
            def _():
                act(relay(part, source * 2 + lane, to))

    if square:

        @pl.when((chip == 0) & (core == 0))
        def _():
            for part in range(2):
                arrived(part, 2)
                relay(part, 2, 2).start()

    def nth(i):
        if square:
            return jnp.where(chip == 3, lax.rem(i + 1, 3), i)
        return chip - 1 - i

    def chip_step(i, carry):
        other = nth(i)
        for part in range(2):
            arrived(part, other * 2 + core)
            if square:
                each_relay(other, part, lambda copy: copy.start())
            forward(part, other).start()
        for part in range(2):
            arrived(part, other * 2 + 1 - core)
        step([other * 2, other * 2 + 1])
        return carry

    lax.fori_loop(0, chip, chip_step, 0)

    part = jnp.zeros((8, d), jnp.float32)
    for h in range(heads):
        a = acc[h]
        t = (a[:, :d] / a[:, d:]).astype(jnp.bfloat16)
        t_ref[h] = t
        b = sacc[h] + mm(phiq[h], state[h // group].astype(jnp.bfloat16))
        o = (b[:, :d] / b[:, d:]).astype(jnp.bfloat16)
        s_ref[h] = o
        diff = t.astype(jnp.float32) - o.astype(jnp.float32)
        part += jnp.sum((diff * diff).reshape(rows // 8, 8, d), axis=0)

    def exchange(slots, me, size, axis, send, recv, value):
        slots[me] = value

        def copy(off):
            return pltpu.make_async_remote_copy(
                src_ref=slots.at[me],
                dst_ref=slots.at[me],
                send_sem=send.at[off],
                recv_sem=recv.at[off],
                device_id={axis: lax.rem(me + off, size)},
                device_id_type=MESH,
            )

        def landed(off):
            src = lax.rem(me + size - off, size)
            pltpu.make_async_remote_copy(
                src_ref=slots.at[src],
                dst_ref=slots.at[src],
                send_sem=send.at[off],
                recv_sem=recv.at[off],
                device_id={axis: lax.rem(me + off, size)},
                device_id_type=MESH,
            ).wait_recv()

        for off in range(1, size):
            copy(off).start()
        for off in range(1, size):
            landed(off)
        total = slots[0]
        for j in range(1, size):
            total = total + slots[j]
        return total, lambda: [copy(off).wait_send() for off in range(1, size)]

    total, end1 = exchange(slots1, p, n, "seq", l1_send, l1_recv, part)
    total, end2 = exchange(slots2, hid, m, "head", l2_send, l2_recv, total)
    loss_ref[0, 0] = jnp.sum(total) * (1.0 / count)

    end1()
    end2()
    each_own(lambda copy: copy.wait_send())

    def sent(i, carry):
        for part in range(2):
            forward(part, i).wait_send()
        return carry

    lax.fori_loop(0, chip, sent, 0)
    if square:
        for who, lane, source, to in relays:

            @pl.when((chip == who) & (core == lane))
            def _():
                for part in range(2):
                    relay(part, source * 2 + lane, to).wait_send()


def local(queries, keys, values, query_map, key_map):
    rows, heads, d = queries.shape
    kvh = keys.shape[1]
    n, m = lax.axis_size("seq"), lax.axis_size("head")
    f = query_map.shape[2]
    count = rows * n * heads * m * d
    vmem = pl.BlockSpec(memory_space=pltpu.VMEM)
    hbm = pl.BlockSpec(memory_space=pl.ANY)
    dma = pltpu.SemaphoreType.DMA
    t, s, loss = pl.pallas_call(
        functools.partial(kernel, n, m, count),
        out_shape=(
            pltpu.VMEM((heads, rows, d), jnp.bfloat16),
            pltpu.VMEM((heads, rows, d), jnp.bfloat16),
            jax.ShapeDtypeStruct((1, 1), jnp.float32),
        ),
        in_specs=[hbm] + [vmem] * 4,
        out_specs=(vmem, vmem, pl.BlockSpec(memory_space=pltpu.SMEM)),
        scratch_shapes=[
            pltpu.VMEM((rows, heads, d), jnp.bfloat16),
            pltpu.VMEM((n, 2, kvh, rows, d), jnp.bfloat16),
            pltpu.VMEM((rows * heads, d), jnp.float32),
            pltpu.VMEM((heads, rows, d), jnp.bfloat16),
            pltpu.VMEM((heads, rows, 2 * f), jnp.bfloat16),
            pltpu.VMEM((heads, rows, d), jnp.float32),
            pltpu.VMEM((heads, rows, 2 * d), jnp.float32),
            pltpu.VMEM((heads, rows, 2 * d), jnp.float32),
            pltpu.VMEM((kvh, 2 * f, 2 * d), jnp.float32),
            pltpu.VMEM((n, 8, d), jnp.float32),
            pltpu.VMEM((m, 8, d), jnp.float32),
            dma((2, n // 2)),
            dma((2, n // 2)),
            dma((2,)),
            dma((1,)),
            dma((2, n)),
            dma((n,)),
            dma((n,)),
            dma((m,)),
            dma((m,)),
        ],
        compiler_params=pltpu.CompilerParams(
            collective_id=0, has_side_effects=True, vmem_limit_bytes=48 * 2**20
        ),
    )(
        queries,
        keys.transpose(1, 0, 2),
        values.transpose(1, 0, 2),
        query_map.transpose(0, 2, 1),
        key_map.transpose(0, 2, 1),
    )
    return t.transpose(1, 0, 2), s.transpose(1, 0, 2), loss.reshape(())


def solution(mesh):
    placed = (
        P("seq", "head", None),
        P("seq", "head", None),
        P("seq", "head", None),
        P("head", None, None),
        P("head", None, None),
    )
    return jax.shard_map(
        local,
        mesh=mesh,
        in_specs=placed,
        out_specs=(P("seq", "head", None), P("seq", "head", None), P()),
        check_vma=False,
    )
```

```python
import functools
import math

import jax
import jax.numpy as jnp
from jax import lax
from jax.experimental import pallas as pl
from jax.experimental.pallas import tpu as pltpu
from jax.sharding import PartitionSpec as P

MESH = pl.DeviceIdType.MESH
NT = (((1,), (1,)), ((), ()))
NN = (((1,), (0,)), ((), ()))
LOW = -1e30


def mm(a, b, dims=NN):
    return lax.dot_general(a, b, dims, preferred_element_type=jnp.float32)


def kernel(
    n,
    m,
    count,
    q_hbm,
    k_ref,
    v_ref,
    qm_ref,
    km_ref,
    t_ref,
    s_ref,
    loss_ref,
    q_ref,
    kvbuf,
    wide,
    qh,
    phiq,
    top,
    acc,
    sacc,
    state,
    slots1,
    slots2,
    send_sem,
    fwd_sem,
    relay_sem,
    local_sem,
    recv_sem,
    l1_send,
    l1_recv,
    l2_send,
    l2_recv,
):
    rows, heads, d = q_ref.shape
    load_q = pltpu.make_async_copy(q_hbm, q_ref, local_sem.at[0])
    load_q.start()
    kvh = k_ref.shape[0]
    group = heads // kvh
    f = qm_ref.shape[1]
    c2 = math.log2(math.e) / math.sqrt(d)
    p = lax.axis_index("seq")
    hid = lax.axis_index("head")
    chip = p // 2
    core = p % 2
    partner = p + 1 - 2 * core
    chips = n // 2
    square = chips == 4

    barrier = pltpu.get_barrier_semaphore()
    for off in range(1, n):
        pl.semaphore_signal(
            barrier, inc=1, device_id={"seq": lax.rem(p + off, n)}, device_id_type=MESH
        )
    for off in range(1, m):
        pl.semaphore_signal(
            barrier, inc=1, device_id={"head": lax.rem(hid + off, m)}, device_id_type=MESH
        )

    def features(x, half_map):
        u = mm(jnp.concatenate([half_map, -half_map], axis=0), x, NT)
        parts = []
        for half in (u[:f], u[f:]):
            e = jnp.exp(half - jnp.max(half, axis=0, keepdims=True))
            parts.append(e * (1.0 / jnp.sum(e, axis=0, keepdims=True)))
        return jnp.concatenate(parts, axis=0)

    load_q.wait()
    wide[...] = q_ref[...].astype(jnp.float32).reshape(rows * heads, d)
    for h in range(heads):
        qh[h] = wide[pl.ds(h, rows, stride=heads), :].astype(jnp.bfloat16)
    for h in range(heads):
        phiq[h] = features(qh[h], qm_ref[h]).T.astype(jnp.bfloat16)

    pl.semaphore_wait(barrier, n - 1 + m - 1)

    def own(part, device, sem):
        return pltpu.make_async_remote_copy(
            src_ref=(k_ref, v_ref)[part],
            dst_ref=kvbuf.at[p, part],
            send_sem=send_sem.at[part, sem],
            recv_sem=recv_sem.at[part, p],
            device_id={"seq": device},
            device_id_type=MESH,
        )

    def forward(part, from_chip):
        block = from_chip * 2 + core
        return pltpu.make_async_remote_copy(
            src_ref=kvbuf.at[block, part],
            dst_ref=kvbuf.at[block, part],
            send_sem=fwd_sem.at[part, from_chip],
            recv_sem=recv_sem.at[part, block],
            device_id={"seq": partner},
            device_id_type=MESH,
        )

    def arrived(part, block):
        pltpu.make_async_remote_copy(
            src_ref=kvbuf.at[block, part],
            dst_ref=kvbuf.at[block, part],
            send_sem=fwd_sem.at[part, 0],
            recv_sem=recv_sem.at[part, block],
            device_id={"seq": partner},
            device_id_type=MESH,
        ).wait_recv()

    def near(to):
        if to == 0:
            return (chip == 1) & (core == 0)
        if to == 3:
            return (chip == 1) | (chip == 2)
        return chip == 0

    def relay(part, block, to_chip):
        return pltpu.make_async_remote_copy(
            src_ref=kvbuf.at[block, part],
            dst_ref=kvbuf.at[block, part],
            send_sem=relay_sem.at[part],
            recv_sem=recv_sem.at[part, block],
            device_id={"seq": to_chip * 2 + core},
            device_id_type=MESH,
        )

    relays = ((0, 0, 1, 2), (1, 0, 0, 3), (2, 1, 0, 3), (3, 1, 1, 2))

    def each_own(act):
        @pl.when(core == 0)
        def _():
            act(own(0, partner, chip))
            act(own(1, partner, chip))

        if square:
            for to in range(4):

                @pl.when(near(to))
                def _():
                    act(own(0, to * 2 + core, to))
                    act(own(1, to * 2 + core, to))

            return

        def body(i, carry):
            act(own(0, i * 2 + core, i))
            act(own(1, i * 2 + core, i))
            return carry

        lax.fori_loop(chip + 1, chips, body, 0)

    each_own(lambda copy: copy.start())

    ones = jnp.ones((rows, d), jnp.bfloat16)

    def key_features(k, g):
        return features(k, km_ref[g]).astype(jnp.bfloat16)

    lower = lax.broadcasted_iota(jnp.int32, (rows, rows), 0) >= lax.broadcasted_iota(
        jnp.int32, (rows, rows), 1
    )
    for g in range(kvh):
        k = k_ref[g]
        v1 = jnp.concatenate([v_ref[g], ones], axis=1)
        phik = key_features(k, g)
        state[g] = jnp.zeros_like(state[g])
        for h in range(g * group, (g + 1) * group):
            q = qh[h]
            s = jnp.where(lower, mm(q, k, NT), LOW)
            high = jnp.max(s, axis=1, keepdims=True)
            w = jnp.exp2((s - high) * c2).astype(jnp.bfloat16)
            top[h] = jnp.broadcast_to(high, (rows, d))
            acc[h] = mm(w, v1)
            a = jnp.where(lower, mm(phiq[h], phik), 0.0).astype(jnp.bfloat16)
            sacc[h] = mm(a, v1)

    def step(blocks):
        for g in range(kvh):
            k = jnp.concatenate([kvbuf[b, 0, g] for b in blocks], axis=0)
            v = jnp.concatenate([kvbuf[b, 1, g] for b in blocks], axis=0)
            v1 = jnp.concatenate([v, jnp.ones_like(v)], axis=1)
            state[g] += mm(key_features(k, g), v1)
            for h in range(g * group, (g + 1) * group):
                s = mm(qh[h], k, NT)
                before = top[h]
                high = jnp.maximum(before, jnp.max(s, axis=1, keepdims=True))
                top[h] = high
                w = jnp.exp2((s - jnp.concatenate([high] * (s.shape[1] // d), axis=1)) * c2)
                fade = jnp.exp2((before - high) * c2)
                acc[h] = acc[h] * jnp.concatenate([fade, fade], axis=1) + mm(
                    w.astype(jnp.bfloat16), v1
                )

    @pl.when(core == 1)
    def _():
        for part in range(2):
            arrived(part, p - 1)
        step([p - 1])

    def each_relay(origin, part, act):
        for who, lane, source, to in relays:

            @pl.when((chip == who) & (core == lane) & (origin == source))
            def _():
                act(relay(part, source * 2 + lane, to))

    if square:

        @pl.when((chip == 0) & (core == 0))
        def _():
            for part in range(2):
                arrived(part, 2)
                relay(part, 2, 2).start()

    def nth(i):
        if square:
            return jnp.where(chip == 3, lax.rem(i + 1, 3), i)
        return chip - 1 - i

    def chip_step(i, carry):
        other = nth(i)
        for part in range(2):
            arrived(part, other * 2 + core)
            if square:
                each_relay(other, part, lambda copy: copy.start())
            forward(part, other).start()
        for part in range(2):
            arrived(part, other * 2 + 1 - core)
        step([other * 2, other * 2 + 1])
        return carry

    lax.fori_loop(0, chip, chip_step, 0)

    part = jnp.zeros((8, d), jnp.float32)
    for h in range(heads):
        a = acc[h]
        t = (a[:, :d] / a[:, d:]).astype(jnp.bfloat16)
        t_ref[h] = t
        b = sacc[h] + mm(phiq[h], state[h // group].astype(jnp.bfloat16))
        o = (b[:, :d] / b[:, d:]).astype(jnp.bfloat16)
        s_ref[h] = o
        diff = t.astype(jnp.float32) - o.astype(jnp.float32)
        part += jnp.sum((diff * diff).reshape(rows // 8, 8, d), axis=0)

    def exchange(slots, me, size, axis, send, recv, value):
        slots[me] = value

        def copy(off):
            return pltpu.make_async_remote_copy(
                src_ref=slots.at[me],
                dst_ref=slots.at[me],
                send_sem=send.at[off],
                recv_sem=recv.at[off],
                device_id={axis: lax.rem(me + off, size)},
                device_id_type=MESH,
            )

        def landed(off):
            src = lax.rem(me + size - off, size)
            pltpu.make_async_remote_copy(
                src_ref=slots.at[src],
                dst_ref=slots.at[src],
                send_sem=send.at[off],
                recv_sem=recv.at[off],
                device_id={axis: lax.rem(me + off, size)},
                device_id_type=MESH,
            ).wait_recv()

        for off in range(1, size):
            copy(off).start()
        for off in range(1, size):
            landed(off)
        total = slots[0]
        for j in range(1, size):
            total = total + slots[j]
        return total, lambda: [copy(off).wait_send() for off in range(1, size)]

    total, end1 = exchange(slots1, p, n, "seq", l1_send, l1_recv, part)
    total, end2 = exchange(slots2, hid, m, "head", l2_send, l2_recv, total)
    loss_ref[0, 0] = jnp.sum(total) * (1.0 / count)

    end1()
    end2()
    each_own(lambda copy: copy.wait_send())

    def sent(i, carry):
        for part in range(2):
            forward(part, i).wait_send()
        return carry

    lax.fori_loop(0, chip, sent, 0)
    if square:
        for who, lane, source, to in relays:

            @pl.when((chip == who) & (core == lane))
            def _():
                for part in range(2):
                    relay(part, source * 2 + lane, to).wait_send()


def local(queries, keys, values, query_map, key_map):
    rows, heads, d = queries.shape
    kvh = keys.shape[1]
    n, m = lax.axis_size("seq"), lax.axis_size("head")
    f = query_map.shape[2]
    count = rows * n * heads * m * d
    vmem = pl.BlockSpec(memory_space=pltpu.VMEM)
    hbm = pl.BlockSpec(memory_space=pl.ANY)
    dma = pltpu.SemaphoreType.DMA
    t, s, loss = pl.pallas_call(
        functools.partial(kernel, n, m, count),
        out_shape=(
            pltpu.VMEM((heads, rows, d), jnp.bfloat16),
            pltpu.VMEM((heads, rows, d), jnp.bfloat16),
            jax.ShapeDtypeStruct((1, 1), jnp.float32),
        ),
        in_specs=[hbm] + [vmem] * 4,
        out_specs=(vmem, vmem, pl.BlockSpec(memory_space=pltpu.SMEM)),
        scratch_shapes=[
            pltpu.VMEM((rows, heads, d), jnp.bfloat16),
            pltpu.VMEM((n, 2, kvh, rows, d), jnp.bfloat16),
            pltpu.VMEM((rows * heads, d), jnp.float32),
            pltpu.VMEM((heads, rows, d), jnp.bfloat16),
            pltpu.VMEM((heads, rows, 2 * f), jnp.bfloat16),
            pltpu.VMEM((heads, rows, d), jnp.float32),
            pltpu.VMEM((heads, rows, 2 * d), jnp.float32),
            pltpu.VMEM((heads, rows, 2 * d), jnp.float32),
            pltpu.VMEM((kvh, 2 * f, 2 * d), jnp.float32),
            pltpu.VMEM((n, 8, d), jnp.float32),
            pltpu.VMEM((m, 8, d), jnp.float32),
            dma((2, n // 2)),
            dma((2, n // 2)),
            dma((2,)),
            dma((1,)),
            dma((2, n)),
            dma((n,)),
            dma((n,)),
            dma((m,)),
            dma((m,)),
        ],
        compiler_params=pltpu.CompilerParams(
            collective_id=0, has_side_effects=True, vmem_limit_bytes=61 * 2**20
        ),
    )(
        queries,
        keys.transpose(1, 0, 2),
        values.transpose(1, 0, 2),
        query_map.transpose(0, 2, 1),
        key_map.transpose(0, 2, 1),
    )
    return t.transpose(1, 0, 2), s.transpose(1, 0, 2), loss.reshape(())


def solution(mesh):
    placed = (
        P("seq", "head", None),
        P("seq", "head", None),
        P("seq", "head", None),
        P("head", None, None),
        P("head", None, None),
    )
    return jax.shard_map(
        local,
        mesh=mesh,
        in_specs=placed,
        out_specs=(P("seq", "head", None), P("seq", "head", None), P()),
        check_vma=False,
    )
```
